32 devices in a mesh: blk: 4 (over x, core), grp: 8 (over z, y).
Axes of the slice: x: 2, y: 2, z: 4, core: 2. Of those that a mesh axis runs over, the one named last changes fastest.
Arguments:
- picture_vectors: bfloat16 [12288, 1152], P(('blk', 'grp')), may hold values from -2.3570226 to 2.3570226
- text_vectors: bfloat16 [12288, 1152], P(('blk', 'grp')), may hold values from -2.3570226 to 2.3570226
- matching_text_position: int32 [32, 384], P(('blk', 'grp')), may hold values from 0 to 383, each once within a row
- natural_scale_exponent: float32 [1], replicated, may hold values from 1.5 to 2.3
- offset_added_before_sigmoid: float32 [1], replicated, may hold values from -3 to -1
Outputs:
- image_grad: bfloat16 [12288, 1152], P(('blk', 'grp'))
- caption_grad: bfloat16 [12288, 1152], P(('blk', 'grp'))
The draws below stay inside these ranges and needn't reach their ends.
Inputs may be any that keep to these rules, and one draw needn't show every extreme that they name: `matching_text_position`: each row of positives names every position 0 .. 383 exactly once.
All inputs are finite; a program needn't handle non-finite values.
Results may differ from the reference program's by a relative error of at most 0.0059.
Values may be sent and summed in bfloat16 or wider, within the bound.
A program may use at most 64 MiB of HBM per device.

```python
import math
import jax
import jax.numpy as jnp
from jax import lax

D = 1152
PAIRS = 384
STEPS = 4
BLOCKS = 32
ROWS = 12288


def embedding_draw(key):
    key_rows, key_cols, key_base = jax.random.split(key, 3)
    row_scale = jnp.exp(jax.random.uniform(key_rows, (ROWS, 1), jnp.float32, 0.0, math.log(10.0)))
    col_scale = jnp.exp(jax.random.uniform(key_cols, (1, D), jnp.float32, 0.0, math.log(10.0)))
    base_draw = jax.random.normal(key_base, (ROWS, D), jnp.float32)
    base_draw = jnp.clip(base_draw, -4.0, 4.0)
    values = base_draw * row_scale * col_scale * (0.2 / math.sqrt(D))
    return values.astype(jnp.bfloat16)


def draw_picture_vectors(key, part):
    return embedding_draw(jax.random.fold_in(key, 11))


def draw_text_vectors(key, part):
    return embedding_draw(jax.random.fold_in(key, 23))


def setup_inputs(seed: int = 0) -> dict:
    key_of = jax.random.split(jax.random.key(seed), 6)
    return {
        "picture_vectors": draw_picture_vectors(jax.random.fold_in(key_of[5], 71), 0),
        "text_vectors": draw_text_vectors(jax.random.fold_in(key_of[5], 71), 0),
        "matching_text_position": jax.vmap(lambda own: jax.random.permutation(own, PAIRS))(jax.random.split(key_of[2], BLOCKS)).reshape((BLOCKS, PAIRS)).astype(jnp.int32),
        "natural_scale_exponent": jnp.clip(jax.random.uniform(key_of[3], (1,), jnp.float32, 1.5, 2.3), 1.5, 2.3),
        "offset_added_before_sigmoid": jnp.clip(jax.random.uniform(key_of[4], (1,), jnp.float32, -3.0, -1.0), -3.0, -1.0),
    }


def unit_rows(raw_rows):
    values = raw_rows.astype(jnp.float32)
    inverse_norm = lax.rsqrt(lax.optimization_barrier(jnp.sum(values * values, axis=1, keepdims=True)) + 1e-06)
    return (values * inverse_norm, inverse_norm)

def unit_block(raw_rows):
    return unit_rows(raw_rows)[0].astype(jnp.bfloat16)

def cross_dot_products(picture_entry_slab, window_width_along_diagonal, exponentiated_scale, rotation_offset):
    cosine_table = lax.dot_general(picture_entry_slab, window_width_along_diagonal, (((1,), (1,)), ((), ())), preferred_element_type=jnp.float32)
    return exponentiated_scale * cosine_table + rotation_offset

def sigmoid_cost_coefficients(agreement_table, label_polarity, exponentiated_scale):
    derivative_wrt_presigmoid = -label_polarity * jax.nn.sigmoid(-label_polarity * agreement_table)
    return (exponentiated_scale * derivative_wrt_presigmoid).astype(jnp.bfloat16)

def finish(unit_flat, inverse_norm, direction):
    cosine_table = lax.optimization_barrier(jnp.sum(unit_flat * direction, axis=1, keepdims=True))
    return (inverse_norm * (direction - unit_flat * cosine_table)).astype(jnp.bfloat16)

def reference(picture_vectors, text_vectors, matching_text_position, natural_scale_exponent, offset_added_before_sigmoid):
    exponentiated_scale = jnp.exp(natural_scale_exponent[0])
    rotation_offset = offset_added_before_sigmoid[0]
    midpoint_entries = PAIRS // 2
    image_blocks = picture_vectors.reshape(BLOCKS, PAIRS, D)
    caption_blocks = text_vectors.reshape(BLOCKS, PAIRS, D)
    image_units = lax.map(unit_block, image_blocks)
    caption_units = lax.map(unit_block, caption_blocks)
    columns = lax.broadcasted_iota(jnp.int32, (PAIRS, PAIRS), 1)

    def image_block(block_index):
        device_picture_vectors = image_units[block_index]
        first_labels = jnp.where(columns == matching_text_position[block_index][:, None], 1.0, -1.0).astype(jnp.float32)
        running = jnp.zeros((PAIRS, D), jnp.float32)
        for rotation in range(STEPS):
            upper_half = caption_units[(block_index - rotation) % BLOCKS][:midpoint_entries]
            lower_half = caption_units[(block_index + rotation) % BLOCKS][midpoint_entries:]
            window_width_along_diagonal = jnp.concatenate([upper_half, lower_half], axis=0)
            label_polarity = first_labels if rotation == 0 else -1.0
            coupling_coefficient = sigmoid_cost_coefficients(cross_dot_products(device_picture_vectors, window_width_along_diagonal, exponentiated_scale, rotation_offset), label_polarity, exponentiated_scale)
            running = running + jnp.dot(coupling_coefficient, window_width_along_diagonal, preferred_element_type=jnp.float32)
        unit_flat, inverse_norm = unit_rows(image_blocks[block_index])
        return finish(unit_flat, inverse_norm, running)

    def caption_block(block_index):
        device_text_vectors = caption_units[block_index]
        first_labels = jnp.where(columns == matching_text_position[block_index][:, None], 1.0, -1.0).astype(jnp.float32)
        upper_sum = jnp.zeros((midpoint_entries, D), jnp.float32)
        lower_sum = jnp.zeros((midpoint_entries, D), jnp.float32)
        for rotation in range(STEPS):
            above_adjacent_picture_vectors = image_units[(block_index + rotation) % BLOCKS]
            below_adjacent_picture_vectors = image_units[(block_index - rotation) % BLOCKS]
            above_label_polarity = first_labels[:, :midpoint_entries] if rotation == 0 else -1.0
            below_label_polarity = first_labels[:, midpoint_entries:] if rotation == 0 else -1.0
            above_coupling_coefficient = sigmoid_cost_coefficients(cross_dot_products(above_adjacent_picture_vectors, device_text_vectors[:midpoint_entries], exponentiated_scale, rotation_offset), above_label_polarity, exponentiated_scale)
            below_coupling_coefficient = sigmoid_cost_coefficients(cross_dot_products(below_adjacent_picture_vectors, device_text_vectors[midpoint_entries:], exponentiated_scale, rotation_offset), below_label_polarity, exponentiated_scale)
            upper_sum = upper_sum + lax.dot_general(above_coupling_coefficient, above_adjacent_picture_vectors, (((0,), (0,)), ((), ())), preferred_element_type=jnp.float32)
            lower_sum = lower_sum + lax.dot_general(below_coupling_coefficient, below_adjacent_picture_vectors, (((0,), (0,)), ((), ())), preferred_element_type=jnp.float32)
        direction = jnp.concatenate([upper_sum, lower_sum], axis=0)
        unit_flat, inverse_norm = unit_rows(caption_blocks[block_index])
        return finish(unit_flat, inverse_norm, direction)
    block_ids = jnp.arange(BLOCKS, dtype=jnp.int32)
    image_grad = lax.map(image_block, block_ids).reshape(ROWS, D)
    caption_grad = lax.map(caption_block, block_ids).reshape(ROWS, D)
    return (image_grad, caption_grad)
```

```python
import functools

import jax
import jax.numpy as jnp
from jax import lax
from jax.experimental import pallas as pl
from jax.experimental.pallas import tpu as pltpu
from jax.sharding import PartitionSpec as P

CHUNKS = 2
NORM_ROWS = 48
MESH = pl.DeviceIdType.MESH

A0, A1, A2, A3, B0, B1, B2, B3 = range(8)
(
    OWN_A_PAIR,
    OWN_A_FAR,
    A1_FAR,
    A2_PAIR,
    OWN_B_FAR,
    B2_PAIR,
    SUM_B1,
    SUM_B3,
    SUM_A3,
    SUM_A1,
    SUM_A2,
    SUM_B2,
) = range(12)


def kernel(
    groups,
    total,
    image_ref,
    text_ref,
    position_ref,
    exponent_ref,
    offset_ref,
    image_out,
    text_out,
    image_unit,
    captions,
    coefs,
    partial,
    staged,
    returned,
    direction,
    image_inverse,
    text_inverse,
    send_sem,
    recv_sem,
):
    rows, width = image_ref.shape
    half = rows // 2
    chunk = half // CHUNKS
    me = lax.axis_index("blk") * groups + lax.axis_index("grp")
    parity = lax.rem(me, 2)
    step = 1 - 2 * parity

    def place(index):
        index = lax.rem(index + total, total)
        return (index // groups, lax.rem(index, groups))

    pair = place(me + step)
    ahead = place(me + 2 * step)
    behind = place(me - 2 * step)

    barrier = pltpu.get_barrier_semaphore()
    for device in (pair, ahead, behind):
        pl.semaphore_signal(barrier, inc=1, device_id=device, device_id_type=MESH)

    start_a = pl.multiple_of(parity * half, half)
    start_b = pl.multiple_of(half - parity * half, half)

    def piece(c):
        return pl.ds(c * chunk, chunk)

    def message(name, c, source, target, device):
        return pltpu.make_async_remote_copy(
            src_ref=source.at[piece(c)],
            dst_ref=target.at[piece(c)],
            send_sem=send_sem.at[name, c],
            recv_sem=recv_sem.at[name, c],
            device_id=device,
            device_id_type=MESH,
        )

    routes = {
        OWN_A_PAIR: (captions.at[A0], captions.at[B1], pair),
        OWN_A_FAR: (captions.at[A0], captions.at[A2], ahead),
        A1_FAR: (captions.at[A1], captions.at[A3], ahead),
        A2_PAIR: (captions.at[A2], captions.at[B3], pair),
        OWN_B_FAR: (captions.at[B0], captions.at[B2], behind),
        B2_PAIR: (captions.at[B2], captions.at[A1], pair),
        SUM_B1: (staged.at[0], returned.at[0], pair),
        SUM_B3: (staged.at[1], returned.at[1], pair),
        SUM_A3: (staged.at[2], returned.at[2], behind),
        SUM_A1: (staged.at[3], returned.at[3], pair),
        SUM_A2: (staged.at[4], returned.at[4], behind),
        SUM_B2: (staged.at[5], returned.at[5], ahead),
    }

    def send(name, c):
        message(name, c, *routes[name]).start()

    def receive(name, c):
        message(name, c, *routes[name]).wait_recv()

    def normalize(source, inverse, slot_ref, source_start):
        def body(i, carry):
            at = pl.multiple_of(i * NORM_ROWS, NORM_ROWS)
            here = pl.ds(pl.multiple_of(source_start + at, NORM_ROWS), NORM_ROWS)
            values = source[here, :].astype(jnp.float32)
            scale = lax.rsqrt(jnp.sum(values * values, axis=1, keepdims=True) + 1e-06)
            inverse[here, :] = scale
            slot_ref[pl.ds(at, NORM_ROWS), :] = (values * scale).astype(jnp.bfloat16)
            return carry

        lax.fori_loop(0, slot_ref.shape[0] // NORM_ROWS, body, 0)

    normalize(text_ref, text_inverse, captions.at[B0], start_b)
    normalize(text_ref, text_inverse, captions.at[A0], start_a)
    pl.semaphore_wait(barrier, 3)
    for c in range(CHUNKS):
        send(OWN_B_FAR, c)
        send(OWN_A_FAR, c)
    send(OWN_A_PAIR, 0)
    normalize(image_ref, image_inverse, image_unit, 0)

    scale = jnp.exp(jnp.full((1, rows), exponent_ref[0], jnp.float32))
    offset = offset_ref[0]

    def tile(slot, c, first_row=None):
        text = captions[slot, piece(c), :]
        logit = (
            lax.dot_general(
                text,
                image_unit[...],
                (((1,), (1,)), ((), ())),
                preferred_element_type=jnp.float32,
            )
            * scale
            + offset
        )
        if first_row is None:
            coef = scale * jax.nn.sigmoid(logit)
        else:
            row = lax.broadcasted_iota(jnp.int32, logit.shape, 0) + first_row + c * chunk
            polarity = jnp.where(row == position_ref[0:1, :], 1.0, -1.0)
            coef = scale * (-polarity * jax.nn.sigmoid(-polarity * logit))
        coef = coef.astype(jnp.bfloat16)
        coefs[slot, piece(c), :] = coef
        return jnp.dot(coef, image_unit[...], preferred_element_type=jnp.float32)

    for c in range(CHUNKS):
        receive(OWN_B_FAR, c)
        send(B2_PAIR, c)
        if c + 1 < CHUNKS:
            send(OWN_A_PAIR, c + 1)
        receive(OWN_A_FAR, c)
        send(A2_PAIR, c)
    for c in range(CHUNKS):
        receive(OWN_A_PAIR, c)
        staged[0, piece(c), :] = tile(B1, c).astype(jnp.bfloat16)
        send(SUM_B1, c)
        receive(B2_PAIR, c)
        send(A1_FAR, c)
    for c in range(CHUNKS):
        partial[0, piece(c), :] = tile(A1, c)
        partial[1, piece(c), :] = tile(A2, c)
        partial[2, piece(c), :] = tile(B2, c)
        receive(A2_PAIR, c)
        staged[1, piece(c), :] = tile(B3, c).astype(jnp.bfloat16)
        send(SUM_B3, c)
    for c in range(CHUNKS):
        receive(A1_FAR, c)
        staged[2, piece(c), :] = tile(A3, c).astype(jnp.bfloat16)
        send(SUM_A3, c)
    for c in range(CHUNKS):
        partial[3, piece(c), :] = tile(A0, c, start_a)
        partial[4, piece(c), :] = tile(B0, c, start_b)
    def relay(name, c, source, buffer, slot, part):
        receive(source, c)
        arrived = returned[buffer, piece(c), :].astype(jnp.float32)
        staged[slot, piece(c), :] = (arrived + partial[part, piece(c), :]).astype(
            jnp.bfloat16
        )
        send(name, c)

    for c in range(CHUNKS):
        relay(SUM_A1, c, SUM_A3, 2, 3, 0)
        relay(SUM_A2, c, SUM_B3, 1, 4, 1)
    for c in range(CHUNKS):
        relay(SUM_B2, c, SUM_A1, 3, 5, 2)

    tile_width = 384 if width % 384 == 0 else 128

    def accumulate(i, carry):
        lanes = pl.ds(pl.multiple_of(i * tile_width, 128), tile_width)
        result = jnp.zeros((rows, tile_width), jnp.float32)
        for slot in range(8):
            result += lax.dot_general(
                coefs[slot],
                captions[slot, :, lanes],
                (((0,), (0,)), ((), ())),
                preferred_element_type=jnp.float32,
            )
        direction[:, lanes] = result
        return carry

    lax.fori_loop(0, width // tile_width, accumulate, 0)

    def finish(source, inverse, here, value):
        scale = inverse[here, :]
        flat = source[here, :].astype(jnp.float32) * scale
        cosine = jnp.sum(flat * value, axis=1, keepdims=True)
        return (scale * (value - flat * cosine)).astype(jnp.bfloat16)

    def finish_images(i, carry):
        here = pl.ds(pl.multiple_of(i * NORM_ROWS, NORM_ROWS), NORM_ROWS)
        image_out[here, :] = finish(image_ref, image_inverse, here, direction[here, :])
        return carry

    lax.fori_loop(0, rows // NORM_ROWS, finish_images, 0)

    def finish_text(c, start, part, buffers):
        def body(i, carry):
            at = pl.multiple_of(c * chunk + i * NORM_ROWS, NORM_ROWS)
            local = pl.ds(at, NORM_ROWS)
            here = pl.ds(pl.multiple_of(start + at, NORM_ROWS), NORM_ROWS)
            value = partial[part, local, :]
            for buffer in buffers:
                value += returned[buffer, local, :].astype(jnp.float32)
            text_out[here, :] = finish(text_ref, text_inverse, here, value)
            return carry

        lax.fori_loop(0, chunk // NORM_ROWS, body, 0)

    for c in range(CHUNKS):
        receive(SUM_B1, c)
        receive(SUM_A2, c)
        finish_text(c, start_a, 3, (0, 4))
    for c in range(CHUNKS):
        receive(SUM_B2, c)
        finish_text(c, start_b, 4, (5,))
    for name in routes:
        for c in range(CHUNKS):
            message(name, c, *routes[name]).wait_send()


def solution(mesh):
    groups = mesh.shape["grp"]
    total = mesh.shape["blk"] * groups

    def local(images, texts, positions, exponent, offset):
        rows, width = images.shape
        half = rows // 2
        vmem = pl.BlockSpec(memory_space=pltpu.VMEM)
        smem = pl.BlockSpec(memory_space=pltpu.SMEM)
        return pl.pallas_call(
            functools.partial(kernel, groups, total),
            out_shape=(
                jax.ShapeDtypeStruct((rows, width), jnp.bfloat16),
                jax.ShapeDtypeStruct((rows, width), jnp.bfloat16),
            ),
            in_specs=[vmem, vmem, vmem, smem, smem],
            out_specs=(vmem, vmem),
            scratch_shapes=[
                pltpu.VMEM((rows, width), jnp.bfloat16),
                pltpu.VMEM((8, half, width), jnp.bfloat16),
                pltpu.VMEM((8, half, rows), jnp.bfloat16),
                pltpu.VMEM((5, half, width), jnp.float32),
                pltpu.VMEM((6, half, width), jnp.bfloat16),
                pltpu.VMEM((6, half, width), jnp.bfloat16),
                pltpu.VMEM((rows, width), jnp.float32),
                pltpu.VMEM((rows, 1), jnp.float32),
                pltpu.VMEM((rows, 1), jnp.float32),
                pltpu.SemaphoreType.DMA((12, CHUNKS)),
                pltpu.SemaphoreType.DMA((12, CHUNKS)),
            ],
            compiler_params=pltpu.CompilerParams(
                collective_id=0, has_side_effects=True, vmem_limit_bytes=48 * 1024 * 1024
            ),
        )(images, texts, positions, exponent, offset)

    shard = P(("blk", "grp"), None)
    return jax.shard_map(
        local,
        mesh=mesh,
        in_specs=(shard, shard, shard, P(), P()),
        out_specs=(shard, shard),
        check_vma=False,
    )
```

```python
import functools

import jax
import jax.numpy as jnp
from jax import lax
from jax.experimental import pallas as pl
from jax.experimental.pallas import tpu as pltpu
from jax.sharding import PartitionSpec as P

CHUNKS = 3
NORM_ROWS = 32
MESH = pl.DeviceIdType.MESH

A0, A1, A2, A3, B0, B1, B2, B3 = range(8)
(
    OWN_A_PAIR,
    OWN_A_FAR,
    A1_FAR,
    A2_PAIR,
    OWN_B_FAR,
    B2_PAIR,
    SUM_B1,
    SUM_B3,
    SUM_A3,
    SUM_A1,
    SUM_A2,
    SUM_B2,
) = range(12)


def kernel(
    groups,
    total,
    image_hbm,
    text_hbm,
    position_hbm,
    exponent_ref,
    offset_ref,
    image_out,
    text_out,
    image_ref,
    text_ref,
    position_ref,
    image_unit,
    captions,
    coefs,
    partial,
    staged,
    returned,
    direction,
    image_inverse,
    text_inverse,
    load_sem,
    send_sem,
    recv_sem,
):
    rows, width = image_hbm.shape
    half = rows // 2
    chunk = half // CHUNKS
    me = lax.axis_index("blk") * groups + lax.axis_index("grp")
    parity = lax.rem(me, 2)
    step = 1 - 2 * parity

    def place(index):
        index = lax.rem(index + total, total)
        return (index // groups, lax.rem(index, groups))

    pair = place(me + step)
    ahead = place(me + 2 * step)
    behind = place(me - 2 * step)

    barrier = pltpu.get_barrier_semaphore()
    for device in (pair, ahead, behind):
        pl.semaphore_signal(barrier, inc=1, device_id=device, device_id_type=MESH)

    start_a = pl.multiple_of(parity * half, half)
    start_b = pl.multiple_of(half - parity * half, half)

    def load(n, source, target):
        return pltpu.make_async_copy(source, target, load_sem.at[n])

    half_a, half_b = (pl.ds(start_a, half), pl.ds(start_b, half))
    loads = (
        load(0, text_hbm.at[half_b], text_ref.at[half_b]),
        load(1, text_hbm.at[half_a], text_ref.at[half_a]),
        load(2, image_hbm, image_ref),
        load(3, position_hbm, position_ref),
    )
    for copy in loads:
        copy.start()

    def piece(c):
        return pl.ds(c * chunk, chunk)

    def message(name, c, source, target, device):
        return pltpu.make_async_remote_copy(
            src_ref=source.at[piece(c)],
            dst_ref=target.at[piece(c)],
            send_sem=send_sem.at[name, c],
            recv_sem=recv_sem.at[name, c],
            device_id=device,
            device_id_type=MESH,
        )

    routes = {
        OWN_A_PAIR: (captions.at[A0], captions.at[B1], pair),
        OWN_A_FAR: (captions.at[A0], captions.at[A2], ahead),
        A1_FAR: (captions.at[A1], captions.at[A3], ahead),
        A2_PAIR: (captions.at[A2], captions.at[B3], pair),
        OWN_B_FAR: (captions.at[B0], captions.at[B2], behind),
        B2_PAIR: (captions.at[B2], captions.at[A1], pair),
        SUM_B1: (staged.at[0], returned.at[0], pair),
        SUM_B3: (staged.at[1], returned.at[1], pair),
        SUM_A3: (staged.at[2], returned.at[2], behind),
        SUM_A1: (staged.at[3], returned.at[3], pair),
        SUM_A2: (staged.at[4], returned.at[4], behind),
        SUM_B2: (staged.at[5], returned.at[5], ahead),
    }

    def send(name, c):
        message(name, c, *routes[name]).start()

    def receive(name, c):
        message(name, c, *routes[name]).wait_recv()

    def normalize(source, inverse, slot_ref, source_start):
        def body(i, carry):
            at = pl.multiple_of(i * NORM_ROWS, NORM_ROWS)
            here = pl.ds(pl.multiple_of(source_start + at, NORM_ROWS), NORM_ROWS)
            values = source[here, :].astype(jnp.float32)
            scale = lax.rsqrt(jnp.sum(values * values, axis=1, keepdims=True) + 1e-06)
            inverse[here, :] = scale
            slot_ref[pl.ds(at, NORM_ROWS), :] = (values * scale).astype(jnp.bfloat16)
            return carry

        lax.fori_loop(0, slot_ref.shape[0] // NORM_ROWS, body, 0)

    loads[0].wait()
    normalize(text_ref, text_inverse, captions.at[B0], start_b)
    pl.semaphore_wait(barrier, 3)
    for c in range(CHUNKS):
        send(OWN_B_FAR, c)
    loads[1].wait()
    normalize(text_ref, text_inverse, captions.at[A0], start_a)
    send(OWN_A_PAIR, 0)
    send(OWN_A_FAR, 0)
    for load in loads[2:]:
        load.wait()
    normalize(image_ref, image_inverse, image_unit, 0)

    scale = jnp.exp(jnp.full((1, rows), exponent_ref[0], jnp.float32))
    offset = offset_ref[0]

    def tile(slot, c, first_row=None):
        text = captions[slot, piece(c), :]
        logit = (
            lax.dot_general(
                text,
                image_unit[...],
                (((1,), (1,)), ((), ())),
                preferred_element_type=jnp.float32,
            )
            * scale
            + offset
        )
        if first_row is None:
            coef = scale * jax.nn.sigmoid(logit)
        else:
            row = lax.broadcasted_iota(jnp.int32, logit.shape, 0) + first_row + c * chunk
            polarity = jnp.where(row == position_ref[0:1, :], 1.0, -1.0)
            coef = scale * (-polarity * jax.nn.sigmoid(-polarity * logit))
        coef = coef.astype(jnp.bfloat16)
        coefs[slot, piece(c), :] = coef
        return jnp.dot(coef, image_unit[...], preferred_element_type=jnp.float32)

    def relay(name, c, source, buffer, slot, part):
        receive(source, c)
        arrived = returned[buffer, piece(c), :].astype(jnp.float32)
        staged[slot, piece(c), :] = (arrived + partial[part, piece(c), :]).astype(
            jnp.bfloat16
        )
        send(name, c)

    tile_width = 384 if width % 384 == 0 else 128

    def accumulate(i, carry):
        lanes = pl.ds(pl.multiple_of(i * tile_width, 128), tile_width)
        result = jnp.zeros((rows, tile_width), jnp.float32)
        for slot in range(8):
            result += lax.dot_general(
                coefs[slot],
                captions[slot, :, lanes],
                (((0,), (0,)), ((), ())),
                preferred_element_type=jnp.float32,
            )
        direction[:, lanes] = result
        return carry

    def finish(source, inverse, here, value):
        scale = inverse[here, :]
        flat = source[here, :].astype(jnp.float32) * scale
        cosine = jnp.sum(flat * value, axis=1, keepdims=True)
        return (scale * (value - flat * cosine)).astype(jnp.bfloat16)

    def finish_images(i, carry):
        here = pl.ds(pl.multiple_of(i * NORM_ROWS, NORM_ROWS), NORM_ROWS)
        image_out[here, :] = finish(image_ref, image_inverse, here, direction[here, :])
        return carry


    def finish_text(c, start, part, buffers):
        def body(i, carry):
            at = pl.multiple_of(c * chunk + i * NORM_ROWS, NORM_ROWS)
            local = pl.ds(at, NORM_ROWS)
            here = pl.ds(pl.multiple_of(start + at, NORM_ROWS), NORM_ROWS)
            value = partial[part, local, :]
            for buffer in buffers:
                value += returned[buffer, local, :].astype(jnp.float32)
            text_out[here, :] = finish(text_ref, text_inverse, here, value)
            return carry

        lax.fori_loop(0, chunk // NORM_ROWS, body, 0)

    def forward(arrival, name, c):
        receive(arrival, c)
        send(name, c)

    def keep(slot, part, c, first_row=None):
        partial[part, piece(c), :] = tile(slot, c, first_row)

    def give(arrival, slot, stage, c):
        receive(arrival, c)
        staged[stage, piece(c), :] = tile(slot, c).astype(jnp.bfloat16)

    def images():
        lax.fori_loop(0, width // tile_width, accumulate, 0)
        lax.fori_loop(0, rows // NORM_ROWS, finish_images, 0)

    for c in range(CHUNKS):
        forward(OWN_B_FAR, B2_PAIR, c)
        if c + 1 < CHUNKS:
            send(OWN_A_FAR, c + 1)
            send(OWN_A_PAIR, c + 1)
    for c in range(CHUNKS):
        forward(B2_PAIR, A1_FAR, c)
        forward(OWN_A_FAR, A2_PAIR, c)
    give(OWN_A_PAIR, B1, 0, 0)
    send(SUM_B1, 0)
    for c in range(1, CHUNKS):
        give(OWN_A_PAIR, B1, 0, c)

    for c in range(CHUNKS):
        keep(A1, 0, c)
        give(A1_FAR, A3, 2, c)
        send(SUM_A3, c)
        give(A2_PAIR, B3, 1, c)
        send(SUM_B3, c)
    for c in range(CHUNKS):
        keep(A2, 1, c)
        keep(B2, 2, c)

    for c in range(CHUNKS):
        relay(SUM_A1, c, SUM_A3, 2, 3, 0)
        relay(SUM_A2, c, SUM_B3, 1, 4, 1)
    for c in range(1, CHUNKS):
        send(SUM_B1, c)

    for c in range(CHUNKS):
        keep(A0, 3, c, start_a)
        keep(B0, 4, c, start_b)

    for c in range(CHUNKS):
        relay(SUM_B2, c, SUM_A1, 3, 5, 2)

    images()

    for c in range(CHUNKS):
        receive(SUM_B1, c)
        receive(SUM_A2, c)
        finish_text(c, start_a, 3, (0, 4))
    for c in range(CHUNKS):
        receive(SUM_B2, c)
        finish_text(c, start_b, 4, (5,))

    for name in routes:
        for c in range(CHUNKS):
            message(name, c, *routes[name]).wait_send()


def solution(mesh):
    groups = mesh.shape["grp"]
    total = mesh.shape["blk"] * groups

    def local(images, texts, positions, exponent, offset):
        rows, width = images.shape
        half = rows // 2
        vmem = pl.BlockSpec(memory_space=pltpu.VMEM)
        hbm = pl.BlockSpec(memory_space=pl.ANY)
        smem = pl.BlockSpec(memory_space=pltpu.SMEM)
        return pl.pallas_call(
            functools.partial(kernel, groups, total),
            out_shape=(
                jax.ShapeDtypeStruct((rows, width), jnp.bfloat16),
                jax.ShapeDtypeStruct((rows, width), jnp.bfloat16),
            ),
            in_specs=[hbm, hbm, hbm, smem, smem],
            out_specs=(vmem, vmem),
            scratch_shapes=[
                pltpu.VMEM((rows, width), jnp.bfloat16),
                pltpu.VMEM((rows, width), jnp.bfloat16),
                pltpu.VMEM((1, rows), jnp.int32),
                pltpu.VMEM((rows, width), jnp.bfloat16),
                pltpu.VMEM((8, half, width), jnp.bfloat16),
                pltpu.VMEM((8, half, rows), jnp.bfloat16),
                pltpu.VMEM((5, half, width), jnp.float32),
                pltpu.VMEM((6, half, width), jnp.bfloat16),
                pltpu.VMEM((6, half, width), jnp.bfloat16),
                pltpu.VMEM((rows, width), jnp.float32),
                pltpu.VMEM((rows, 1), jnp.float32),
                pltpu.VMEM((rows, 1), jnp.float32),
                pltpu.SemaphoreType.DMA((4,)),
                pltpu.SemaphoreType.DMA((12, CHUNKS)),
                pltpu.SemaphoreType.DMA((12, CHUNKS)),
            ],
            compiler_params=pltpu.CompilerParams(
                collective_id=0, has_side_effects=True, vmem_limit_bytes=60 * 1024 * 1024
            ),
        )(images, texts, positions, exponent, offset)

    shard = P(("blk", "grp"), None)
    return jax.shard_map(
        local,
        mesh=mesh,
        in_specs=(shard, shard, shard, P(), P()),
        out_specs=(shard, shard),
        check_vma=False,
    )
```
